32 devices in a mesh: row: 8 (over y, x, core), layer: 4 (over z).
Axes of the slice: x: 2, y: 2, z: 4, core: 2. Of those that a mesh axis runs over, the one named last changes fastest.
Arguments:
- panel_left: bfloat16 [8, 8, 2048, 128], P('row', 'layer'), may hold values from -6 to 6
- panel_right: bfloat16 [8, 8, 2048, 128], P('row', 'layer'), may hold values from -0.125 to 0.125
- test_matrix: bfloat16 [2048, 128], replicated, may hold values from -6 to 6
- ranks: int32 [8, 8], P('row', 'layer'), may hold values from 32 to 128, as said below
- offsets: int32 [8, 2], P('row'), may hold values from 1 to 4, as said below
Outputs:
- basis: float32 [8, 2048, 2, 128], P('row', 'layer')
- update_right: float32 [8, 2048, 2, 128], P('row', 'layer')
The draws below stay inside these ranges and needn't reach their ends.
Inputs may be any that keep to these rules, and one draw needn't show every extreme that they name: `ranks`: some tile has rank 128 and some tile has rank 128 // 4. An owner's 2 offsets differ from each other; the values 1 and 4 occur in every draw.
All inputs are finite; a program needn't handle non-finite values.
Results may differ from the reference program's by a relative error of at most 0.0003.
Values may be sent and summed in bfloat16 or wider, within the bound.
No kernel may reach another device: no remote copies, remote signals or barrier semaphores. Data moves between devices by JAX's collectives and lax.ppermute only.
A program may use at most 64 MiB of HBM per device.

```python
import jax
import jax.numpy as jnp
from jax import lax

B = 2048
R = 128
FRONTS = 4
TARGETS = 2
OWNERS = 8
LAYERS = 8


def draw_ranks(key, part):
    draws_all = jax.random.randint(key, (OWNERS, LAYERS), R // 4, R + 1, dtype=jnp.int32)
    return draws_all.at[0, 0].set(R).at[0, 1].set(R // 4)


def draw_offsets(key, part):
    row_keys = jax.random.split(jax.random.fold_in(key, 7), OWNERS)
    orders = jax.vmap(lambda row_key: jax.random.permutation(row_key, FRONTS))(row_keys)
    picked = orders[:, :TARGETS].astype(jnp.int32) + 1
    return picked.at[0].set(jnp.array([1, FRONTS], dtype=jnp.int32))


def levels(key, dims, shards, smallest, high):
    gain, own = 1.0, jax.random.fold_in(key, 6)
    for position, blocks in shards:
        heights = jnp.exp(jax.random.uniform(jax.random.fold_in(own, position), (blocks,), jnp.float32, smallest / len(shards), high / len(shards)))
        gain = gain * jnp.repeat(heights, dims[position] // blocks).reshape([-1 if axis == position else 1 for axis in range(len(dims))])
    return gain


def centred(stream_key, extent, width, limit, shards=(), held_as=jnp.bfloat16):
    gain = levels(stream_key, extent, shards, -0.22, 0.18) if shards else 1.0
    values = jax.random.normal(stream_key, extent, jnp.float32) * width * gain
    return jnp.minimum(jnp.maximum(values, -limit), limit).astype(held_as)


def setup_inputs(seed: int = 0) -> dict:
    streams_of = jax.random.split(jax.random.key(seed), 6)
    return {
        "panel_left": centred(streams_of[0], (OWNERS, LAYERS, B, R), 1.0, 6.0, ((0, 8), (1, 4))),
        "panel_right": centred(streams_of[1], (OWNERS, LAYERS, B, R), B ** -0.5, 0.125, ((0, 8), (1, 4))),
        "test_matrix": centred(streams_of[2], (B, R), 1.0, 6.0),
        "ranks": draw_ranks(jax.random.fold_in(streams_of[5], 71), 0),
        "offsets": draw_offsets(jax.random.fold_in(streams_of[5], 71), 0),
    }


def orthonormal(sketch_rows, gram_mat):
    factor = jnp.linalg.cholesky(gram_mat)
    by_cols = jnp.transpose(sketch_rows, (1, 2, 0))
    solved = lax.linalg.triangular_solve(factor, by_cols, left_side=True, lower=True)
    return jnp.transpose(solved, (2, 0, 1))

def reference(panel_left, panel_right, test_matrix, ranks, offsets):
    columns = jnp.arange(R, dtype=jnp.int32)
    high = lax.Precision.HIGHEST
    test_full = test_matrix.astype(jnp.float32)

    def masked(owner_idx):
        live_cols = (columns[None, :] < ranks[owner_idx][:, None]).astype(jnp.bfloat16)
        own_left = lax.dynamic_index_in_dim(panel_left, owner_idx, 0, keepdims=False) * live_cols[:, None, :]
        own_right = lax.dynamic_index_in_dim(panel_right, owner_idx, 0, keepdims=False) * live_cols[:, None, :]
        return (own_left.astype(jnp.float32), own_right.astype(jnp.float32))

    def per_owner(owner_idx):
        own_left, own_right = masked(owner_idx)
        cores = []
        mixers = []
        partners = []
        for target in range(TARGETS):
            partner = ((owner_idx - offsets[owner_idx, target]) % OWNERS).astype(jnp.int32)
            other_left, other_right = masked(partner)
            core_mat = jnp.einsum('kbr,kbq->krq', own_right, other_right, precision=high)
            probes = jnp.einsum('kbr,bq->krq', other_left, test_full, precision=high)
            mix_mat = jnp.einsum('krq,kqs->krs', core_mat, probes, precision=high)
            cores.append(core_mat)
            mixers.append(mix_mat)
            partners.append(other_left)
        mixed = jnp.stack(mixers, axis=1)
        total_sketch = jnp.einsum('kbr,ksrq->bsq', own_left, mixed, precision=high)
        gram_mat = jnp.einsum('bsr,bsq->srq', total_sketch, total_sketch, precision=high) / B
        basis_part = orthonormal(total_sketch, gram_mat)
        reach = jnp.einsum('kbr,bsq->ksrq', own_left, basis_part, precision=high)
        term_list = []
        for target in range(TARGETS):
            weights = jnp.einsum('krq,krs->kqs', cores[target], reach[:, target], precision=high)
            term_list.append(jnp.einsum('kbq,kqs->bs', partners[target], weights, precision=high))
        update_part = jnp.stack(term_list, axis=1) / B
        return (basis_part, update_part)
    basis, update_right = lax.map(per_owner, jnp.arange(OWNERS, dtype=jnp.int32))
    return (basis, update_right)
```

```python
import functools

import jax
import jax.numpy as jnp
from jax import lax
from jax.experimental import pallas as pl
from jax.experimental.pallas import tpu as pltpu
from jax.sharding import PartitionSpec as P

FRONTS = 4
TARGETS = 2
PAIR = 2
MOST = 4
HIGH = lax.Precision.HIGHEST
F32 = jnp.float32
BF16 = jnp.bfloat16


def dot0(a, b, precision=None):
    return lax.dot_general(
        a, b, (((0,), (0,)), ((), ())), precision=precision, preferred_element_type=F32
    )


def split3(x):
    top = x.astype(BF16)
    rest = x - top.astype(F32)
    mid = rest.astype(BF16)
    low = (rest - mid.astype(F32)).astype(BF16)
    return top, mid, low


def wide3(x):
    return jnp.concatenate(split3(x), axis=-1)


def fold3(acc):
    width = acc.shape[-1] // 3
    return (acc[:, 2 * width :] + acc[:, width : 2 * width]) + acc[:, :width]


def call(body, outs, scratch=(), smem=0, n_in=0, name=None):
    specs = [pl.BlockSpec(memory_space=pltpu.SMEM)] * smem
    specs += [pl.BlockSpec(memory_space=pltpu.VMEM)] * (n_in - smem)
    return pl.pallas_call(
        body,
        out_shape=outs,
        in_specs=specs,
        out_specs=jax.tree.map(lambda _: pl.BlockSpec(memory_space=pltpu.VMEM), outs),
        scratch_shapes=list(scratch),
        compiler_params=pltpu.CompilerParams(vmem_limit_bytes=56 << 20),
        name=name,
    )


def core_body(idx, v0, v1, x0, x1, y0, y1, p0, p1, px, py, out, cores, probes):
    cap = v0.shape[-1]
    both = jnp.concatenate([v0[...], v1[...]], axis=1)
    inner = dot0(v0[...], v1[...])
    cores[0, 1] = inner
    cores[1, 0] = inner.T
    for slot, (left, right) in ((2, (x0, x1)), (4, (y0, y1))):
        prod = dot0(both, jnp.concatenate([left[...], right[...]], axis=1))
        for owner in range(PAIR):
            for side in range(PAIR):
                cores[owner, slot + side] = prod[
                    owner * cap : (owner + 1) * cap, side * cap : (side + 1) * cap
                ]
    probes[0] = p0[...]
    probes[1] = p1[...]
    for side in range(PAIR):
        probes[2 + side] = px[side]
        probes[4 + side] = py[side]
    for owner in range(PAIR):
        for target in range(TARGETS):
            tile = idx[owner * TARGETS + target]
            core = cores[owner, tile]
            cols = slice(target * cap, (target + 1) * cap)
            out[owner, 1, :, cols] = core
            out[owner, 0, :, cols] = jnp.dot(
                core, probes[tile], precision=HIGH, preferred_element_type=F32
            )


def sketch_body(count, *refs):
    lefts, mixers = refs[:count], refs[count : 2 * count]
    out3, gram, wide = refs[2 * count :]
    cap = lefts[0].shape[-1]
    tall = lefts[0].shape[1]
    block = min(256, tall)
    for d in range(count):
        for l in range(PAIR):
            wide[d, l * cap : (l + 1) * cap] = wide3(mixers[d][l])
    gram[...] = jnp.zeros_like(gram)

    def step(i, _):
        rows = pl.ds(pl.multiple_of(i * block, block), block)
        acc = jnp.zeros((block, wide.shape[-1]), F32)
        for d in range(count):
            left = jnp.concatenate([lefts[d][0, rows, :], lefts[d][1, rows, :]], axis=1)
            acc += jnp.dot(left, wide[d], preferred_element_type=F32)
        sketch = fold3(acc)
        out3[rows, :] = wide3(sketch)
        for target in range(TARGETS):
            piece = sketch[:, target * cap : (target + 1) * cap]
            gram[target] += dot0(piece, piece, HIGH)
        return 0

    lax.fori_loop(0, tall // block, step, 0)
    gram[...] = gram[...] * (1.0 / tall)


def weight_body(count, *refs):
    lefts, cores = refs[:count], refs[count : 2 * count]
    sketch3, out = refs[2 * count :]
    cap = lefts[0].shape[-1]
    for d in range(count):
        left = jnp.concatenate([lefts[d][0], lefts[d][1]], axis=1)
        reach = fold3(dot0(left, sketch3[...]))
        for l in range(PAIR):
            for target in range(TARGETS):
                cols = slice(target * cap, (target + 1) * cap)
                out[d * PAIR + l, :, cols] = dot0(
                    cores[d][l, :, cols], reach[l * cap : (l + 1) * cap, cols], HIGH
                )


def factor_body(gram, out, work):
    cap = gram.shape[-1]
    panel = 8
    lane = lax.broadcasted_iota(jnp.int32, (cap, cap), 1)
    line = lax.broadcasted_iota(jnp.int32, (cap, cap), 0)
    for target in range(TARGETS):
        work[target, :, :cap] = gram[target]
        work[target, :, cap:] = (lane == line).astype(F32)
    rows8 = lax.broadcasted_iota(jnp.int32, (panel, 1), 0)
    for first in range(0, cap, panel):
        for target in range(TARGETS):
            rows = work[target, first : first + panel, :]
            for i in range(panel):
                column = rows[:, first + i : first + i + 1]
                pivot = column[i : i + 1, :]
                inv = lax.rsqrt(pivot)
                inv = inv * (1.5 - 0.5 * pivot * inv * inv)
                line_i = rows[i : i + 1, :] * inv
                below = jnp.where(rows8 > i, column * inv, 0.0)
                rows = jnp.where(rows8 == i, line_i, rows - below * line_i)
            work[target, first : first + panel, :] = rows
            out[target, first : first + panel, :] = rows[:, cap:]
            if first + panel < cap:
                tail = slice(first + panel, cap)
                work[target, tail, :] = work[target, tail, :] - dot0(rows[:, tail], rows, HIGH)


def slice_body(count, halves, pick, *refs):
    lefts = refs[:count]
    roots = refs[count : 2 * count]
    rests = refs[2 * count : 3 * count - 1]
    cand = refs[3 * count - 1 : 3 * count - 1 + 4 * halves]
    out, chosen = refs[3 * count - 1 + 4 * halves :]
    cap = lefts[0].shape[-1]
    share = lefts[0].shape[1]
    acc = jnp.zeros((share, 3 * TARGETS * cap), F32)
    for d in range(count):
        mix = roots[d][...] if d == 0 else roots[d][...] + rests[d - 1][...]
        wide = wide3(jnp.concatenate([mix[0], mix[1]], axis=0))
        left = jnp.concatenate([lefts[d][0], lefts[d][1]], axis=1)
        acc += jnp.dot(left, wide, preferred_element_type=F32)
    out[...] = fold3(acc)
    per = cand[0].shape[0]
    for target in range(TARGETS):
        for c in range(4):

            @pl.when(pick[target] == c)
            def _():
                for h in range(halves):
                    chosen[target, h * per : (h + 1) * per] = cand[c * halves + h][...]


def final_body(count, parts, place, *refs):
    weights = refs[:parts]
    sketch, chosen, factor, basis, update, total = refs[parts:]
    cap = factor.shape[-1]
    share = sketch.shape[0]
    tall = basis.shape[1] * count
    acc = weights[0][...]
    if parts > 1:
        acc = jnp.where(place[1] == 0, acc, 0.0)
    for d in range(1, parts):
        acc += weights[d][...]
    total[...] = acc
    for target in range(TARGETS):
        cols = slice(target * cap, (target + 1) * cap)
        got = jnp.zeros((share, 3 * cap), F32)
        for d in range(count):
            e = lax.rem(place[1] + d, count)
            wide = wide3(
                jnp.concatenate([total[e * PAIR, :, cols], total[e * PAIR + 1, :, cols]], axis=0)
            )
            left = jnp.concatenate(
                [chosen[target, d * PAIR], chosen[target, d * PAIR + 1]], axis=1
            )
            got += jnp.dot(left, wide, preferred_element_type=F32)
        inverse = factor[target]

        def solve(rows):
            return lax.dot_general(
                rows, inverse, (((1,), (1,)), ((), ())), precision=HIGH, preferred_element_type=F32
            )

        basis[0, :, target, :] = solve(sketch[:, cols])
        update[0, :, target, :] = solve(fold3(got)) * (1.0 / tall)


def on_device(panel_left, panel_right, test_matrix, ranks, offsets):
    n, m = lax.axis_size("row"), lax.axis_size("layer")
    tall, cap = panel_left.shape[2:]
    share = tall // m
    row, z = lax.axis_index("row"), lax.axis_index("layer")
    j = row % PAIR
    roots = [m // 2 - 1 + side for side in range(PAIR)]
    my_root = jnp.where(j == 0, roots[0], roots[1])

    def along(x, shift):
        return lax.ppermute(x, "row", [(i, (i + shift) % n) for i in range(n)])

    def swap(x):
        return lax.ppermute(x, "row", [(i, i ^ 1) for i in range(n)])

    relay = n == 2 * FRONTS

    def group_before(own, two_before):
        if relay:
            sent = jnp.where((row // PAIR) % 2 == 1, two_before, own)
            return lax.ppermute(sent, "row", [(i, i ^ PAIR) for i in range(n)])
        return along(own, PAIR)

    def flat(x, pairs):
        return lax.ppermute(x, ("row", "layer"), [(a * m + b, c * m + d) for a, b, c, d in pairs])

    def to_root(x, d):
        return flat(x, [(r, (roots[r % PAIR] + d) % m, r, roots[r % PAIR]) for r in range(n)])

    def to_rest(x, d):
        return flat(
            x,
            [(r, (k + d) % m, r, k) for r in range(n) for k in range(m) if k != roots[r % PAIR]],
        )

    def from_root(x, d):
        return flat(x, [(r, roots[r % PAIR], r, (roots[r % PAIR] + d) % m) for r in range(n)])

    def doubled(x):
        x = jnp.where(z == my_root, x, 0.0)
        width = 1
        while width < m:
            steps = [(roots[r % PAIR] + e, r) for r in range(n) for e in range(min(width, m - width))]
            x = x + flat(x, [(r, k % m, r, (k + width) % m) for k, r in steps])
            width *= 2
        return x

    columns = lax.broadcasted_iota(jnp.int32, (ranks.shape[1], 1, cap), 2)
    live = (columns < ranks[0][:, None, None]).astype(BF16)
    left = panel_left[0]
    right = panel_right[0] * live

    def mine(x):
        return lax.dynamic_index_in_dim(x, j, 0, keepdims=False)

    def other(x):
        return lax.dynamic_index_in_dim(x, 1 - j, 0, keepdims=False)

    v_own = mine(right)
    v_sib = swap(other(right))
    vy_own, vy_sib = along(v_own, FRONTS), along(v_sib, FRONTS)
    vx_own, vx_sib = group_before(v_own, vy_own), group_before(v_sib, vy_sib)

    probe = jnp.einsum("kbr,bq->krq", left, test_matrix, preferred_element_type=F32)
    note = jnp.pad(offsets.astype(F32), ((0, 7), (0, cap - TARGETS)))
    got = swap(jnp.concatenate([other(probe), note], axis=0))
    p_own, p_sib = mine(probe), got[:cap]
    sib_offsets = got[cap : cap + 1, :TARGETS].astype(jnp.int32)
    p_pair = jnp.stack([p_own, p_sib])
    py = along(p_pair, FRONTS)
    px = group_before(p_pair, py)

    def back(steps, side):
        v = steps - side
        return (v + 1) // PAIR, v % PAIR

    own_group, own_core = back(offsets[0], j)
    sib_group, sib_core = back(sib_offsets[0], 1 - j)
    idx = jnp.concatenate(
        [
            PAIR * own_group + (own_core != j).astype(jnp.int32),
            PAIR * sib_group + (sib_core != j).astype(jnp.int32),
        ]
    ).astype(jnp.int32)

    def piece(at):
        return lax.dynamic_slice_in_dim(left, at * share, share, 1)

    u_rows = [piece(z)]
    for d in range(1, m):
        u_rows.append(
            flat(
                piece((z - d) % m),
                [(r, (k + d) % m, r, k) for r in range(n) for k in range(m)],
            )
        )
    u_root = [left] + [to_root(left, d) for d in range(1, m)]

    pairs = call(
        core_body,
        jax.ShapeDtypeStruct((PAIR, 2, cap, TARGETS * cap), F32),
        [pltpu.VMEM((PAIR, 6, cap, cap), F32), pltpu.VMEM((6, cap, cap), F32)],
        smem=1,
        n_in=11,
        name="cores",
    )(idx, v_own, v_sib, vx_own, vx_sib, vy_own, vy_sib, p_own, p_sib, px, py)
    theirs = swap(pairs[1])
    ordered = jnp.where(
        j == 0, jnp.stack([pairs[0], theirs], axis=1), jnp.stack([theirs, pairs[0]], axis=1)
    )
    mix, core = ordered[0], ordered[1]
    mix_root = [mix] + [to_root(mix, d) for d in range(1, m)]
    core_root = [core] + [to_root(core, d) for d in range(1, m)]
    mix_rest = [to_rest(mix, d) for d in range(1, m)]

    sketch3, gram = call(
        functools.partial(sketch_body, m),
        (
            jax.ShapeDtypeStruct((tall, 3 * TARGETS * cap), BF16),
            jax.ShapeDtypeStruct((TARGETS, cap, cap), F32),
        ),
        [pltpu.VMEM((m, PAIR * cap, 3 * TARGETS * cap), BF16)],
        n_in=2 * m,
        name="sketch",
    )(*u_root, *mix_root)
    is_root = z == my_root
    gram_all = jnp.where(is_root, gram, 0.0)
    for d in range(1, m):
        gram_all = gram_all + from_root(gram, d)
    weights = call(
        functools.partial(weight_body, m),
        jax.ShapeDtypeStruct((m * PAIR, cap, TARGETS * cap), F32),
        n_in=2 * m + 1,
        name="weights",
    )(*u_root, *core_root, sketch3)
    if m <= MOST:
        weight_all = [weights] + [from_root(weights, d) for d in range(1, m)]
    else:
        weight_all = [doubled(weights)]

    factor = call(
        factor_body,
        jax.ShapeDtypeStruct((TARGETS, cap, cap), F32),
        [pltpu.VMEM((TARGETS, cap, 2 * cap), F32)],
        n_in=1,
        name="factor",
    )(gram_all)

    halves = 2
    u_half = [
        jnp.concatenate(u_rows[h * m // halves : (h + 1) * m // halves], axis=0)
        for h in range(halves)
    ]
    uy = [along(u, FRONTS) for u in u_half]
    ux = [group_before(u, y) for u, y in zip(u_half, uy)]
    first = [swap(jnp.where(j == 0, u, y)) for u, y in zip(u_half, uy)]
    second = [swap(x) for x in ux]
    pick = jnp.where(
        own_core == j,
        own_group - 1,
        jnp.where(own_group == 1, 3, 2),
    ).astype(jnp.int32)
    sketch_rows, chosen = call(
        functools.partial(slice_body, m, halves),
        (
            jax.ShapeDtypeStruct((share, TARGETS * cap), F32),
            jax.ShapeDtypeStruct((TARGETS, m * PAIR, share, cap), BF16),
        ),
        smem=1,
        n_in=1 + 3 * m - 1 + 4 * halves,
        name="rows",
    )(pick, *u_rows, *mix_root, *mix_rest, *ux, *uy, *first, *second)

    place = jnp.stack([z, (z - my_root) % m]).astype(jnp.int32)
    out = jax.ShapeDtypeStruct((1, share, TARGETS, cap), F32)
    return call(
        functools.partial(final_body, m, len(weight_all)),
        (out, out),
        [pltpu.VMEM((m * PAIR, cap, TARGETS * cap), F32)],
        smem=1,
        n_in=1 + len(weight_all) + 3,
        name="final",
    )(place, *weight_all, sketch_rows, chosen, factor)


def solution(mesh):
    return jax.shard_map(
        on_device,
        mesh=mesh,
        in_specs=(
            P("row", "layer", None, None),
            P("row", "layer", None, None),
            P(),
            P("row", "layer"),
            P("row", None),
        ),
        out_specs=(P("row", "layer", None, None), P("row", "layer", None, None)),
        check_vma=False,
    )
```

```python
import functools

import jax
import jax.numpy as jnp
from jax import lax
from jax.experimental import pallas as pl
from jax.experimental.pallas import tpu as pltpu
from jax.sharding import PartitionSpec as P


FRONTS = 4
TARGETS = 2
PAIR = 2
MOST = 4
HIGH = lax.Precision.HIGHEST
F32 = jnp.float32
BF16 = jnp.bfloat16


def dot0(a, b, precision=None):
    return lax.dot_general(
        a, b, (((0,), (0,)), ((), ())), precision=precision, preferred_element_type=F32
    )


def dot1(a, b, precision=None):
    return lax.dot_general(
        a, b, (((1,), (1,)), ((), ())), precision=precision, preferred_element_type=F32
    )


def split(x):
    top = x.astype(BF16)
    return top, (x - top.astype(F32)).astype(BF16)


def fold(x, axis):
    first, second = jnp.split(x, 2, axis)
    return first + second


def beside(ref, rows=slice(None), order=(0, 1)):
    return jnp.concatenate([ref[order[0], rows, :], ref[order[1], rows, :]], axis=1)


SMALL = 12 << 20


def call(body, outs, args, scratch=(), smem=0, grant=12 << 20):
    size = sum(a.size * a.dtype.itemsize for a in args)
    size += sum(o.size * o.dtype.itemsize for o in jax.tree.leaves(outs))
    keep = size <= SMALL
    specs = [pl.BlockSpec(memory_space=pltpu.SMEM)] * smem
    specs += [pl.BlockSpec(memory_space=pltpu.VMEM)] * (len(args) - smem)
    if keep:
        args = [
            a if i < smem else pltpu.with_memory_space_constraint(a, pltpu.VMEM)
            for i, a in enumerate(args)
        ]
    return pl.pallas_call(
        body,
        out_shape=outs,
        in_specs=specs,
        out_specs=jax.tree.map(lambda _: pl.BlockSpec(memory_space=pltpu.VMEM), outs),
        scratch_shapes=list(scratch),
        compiler_params=pltpu.CompilerParams(vmem_limit_bytes=grant if keep else 56 << 20),
    )(*args)


def mask_body(info, right, own, other):
    cap = right.shape[-1]
    lane = lax.broadcasted_iota(jnp.int32, (1, cap), 1)
    side = info[PAIR]
    for out, layer in ((own, side), (other, 1 - side)):
        live = (lane < info[layer]).astype(F32).astype(BF16)
        out[...] = right[layer] * live


def probe_body(info, left, test, own, message):
    cap = left.shape[-1]
    side = info[TARGETS]
    own[...] = dot0(left[side], test[...])
    message[:cap] = dot0(left[1 - side], test[...])
    lane = lax.broadcasted_iota(jnp.int32, (8, cap), 1)
    note = jnp.zeros((8, cap), F32)
    for target in range(TARGETS):
        note = jnp.where(lane == target, info[target].astype(F32), note)
    message[cap:] = note


def core_body(idx, v0, v1, x0, x1, y0, y1, p0, p1, px, py, *rest):
    mix_out, core_out, (cores, probes) = rest[:2], rest[2:4], rest[4:]
    cap = v0.shape[-1]
    both = jnp.concatenate([v0[...], v1[...]], axis=1)
    inner = dot0(v0[...], v1[...])
    cores[0, 1] = inner
    cores[1, 0] = inner.T
    for slot, (left, right) in ((4, (y0, y1)), (2, (x0, x1))):
        prod = dot0(both, jnp.concatenate([left[...], right[...]], axis=1))
        for owner in range(PAIR):
            for side in range(PAIR):
                cores[owner, slot + side] = prod[
                    owner * cap : (owner + 1) * cap, side * cap : (side + 1) * cap
                ]
    probes[0] = p0[...]
    probes[1] = p1[:cap, :]
    for side in range(PAIR):
        probes[2 + side] = px[side]
        probes[4 + side] = py[side]
    for owner in range(PAIR):
        for target in range(TARGETS):
            tile = idx[owner * TARGETS + target]
            core = cores[owner, tile]
            cols = slice(target * cap, (target + 1) * cap)
            core_out[owner][:, cols] = core
            mix_out[owner][:, cols] = jnp.dot(
                core, probes[tile], precision=HIGH, preferred_element_type=F32
            )


def sketch_body(count, info, *refs):
    lefts, mixers = refs[:count], refs[count : 2 * count]
    out, gram, wide, whole = refs[2 * count :]
    side = info[0]
    order = (side, 1 - side)
    cap = lefts[0].shape[-1]
    tall = lefts[0].shape[1]
    span = TARGETS * cap
    block = min(512, tall)
    for d in range(count):
        for l in range(PAIR):
            rows = slice((PAIR * d + l) * cap, (PAIR * d + l + 1) * cap)
            wide[rows, :span], wide[rows, span:] = split(mixers[d][l])
    for first in range(0, tall, block):
        rows = slice(first, first + block)
        left = jnp.concatenate([beside(lefts[d], rows, order) for d in range(count)], axis=1)
        sketch = fold(jnp.dot(left, wide[...], preferred_element_type=F32), 1)
        out[rows, :span], out[rows, span:] = split(sketch)
        whole[rows, :] = sketch
    for target in range(TARGETS):
        piece = whole[:, target * cap : (target + 1) * cap]
        gram[target] = dot0(piece, piece, HIGH) * (1.0 / tall)


def weight_body(count, info, *refs):
    lefts, cores = refs[:count], refs[count : 2 * count]
    sketch, out = refs[2 * count :]
    side = info[0]
    cap = lefts[0].shape[-1]
    for d in range(count):
        reach = fold(dot0(sketch[...], beside(lefts[d], order=(side, 1 - side))), 0)
        for l in range(PAIR):
            for target in range(TARGETS):
                cols = slice(target * cap, (target + 1) * cap)
                a0, a1 = split(reach[cols, l * cap : (l + 1) * cap])
                b0, b1 = split(cores[d][l, :, cols])
                out[d * PAIR + l, cols, :] = jnp.dot(
                    jnp.concatenate([a0, a0, a1], axis=1),
                    jnp.concatenate([b0, b1, b0], axis=0),
                    preferred_element_type=F32,
                )


def factor_body(count, *refs):
    grams, (out, work) = refs[:count], refs[count:]
    cap = out.shape[-1]
    panel = 16
    lane = lax.broadcasted_iota(jnp.int32, (cap, cap), 1)
    line = lax.broadcasted_iota(jnp.int32, (cap, cap), 0)
    for target in range(TARGETS):
        gram = grams[0][target]
        for other in grams[1:]:
            gram = gram + other[target]
        work[target, :, :cap] = gram
        work[target, :, cap:] = (lane == line).astype(F32)
    place = lax.broadcasted_iota(jnp.int32, (panel, 1), 0)
    for first in range(0, cap, panel):
        rows = [work[target, first : first + panel, :] for target in range(TARGETS)]
        for i in range(panel):
            for target in range(TARGETS):
                column = rows[target][:, first + i : first + i + 1]
                inv = lax.rsqrt(column[i : i + 1, :])
                line_i = rows[target][i : i + 1, :] * inv
                below = jnp.where(place > i, column * inv, 0.0)
                rows[target] = jnp.where(place == i, line_i, rows[target] - below * line_i)
        for target in range(TARGETS):
            out[target, first : first + panel, :] = rows[target][:, cap:]
            if first + panel < cap:
                tail = slice(first + panel, cap)
                work[target, tail, :] = work[target, tail, :] - dot0(
                    rows[target][:, tail], rows[target], HIGH
                )


def slice_body(count, halves, info, *refs):
    lefts = refs[:count]
    roots = refs[count : 2 * count]
    rests = refs[2 * count : 3 * count - 1]
    cand = refs[3 * count - 1 : 3 * count - 1 + 4 * halves]
    out, chosen = refs[3 * count - 1 + 4 * halves :]
    side = info[TARGETS]
    order = (side, 1 - side)
    parts = []
    for d in range(count):
        mix = roots[d][...] if d == 0 else roots[d][...] + rests[d - 1][...]
        parts.append(jnp.concatenate([mix[0], mix[1]], axis=0))
    wide = jnp.concatenate(split(jnp.concatenate(parts, axis=0)), axis=1)
    left = jnp.concatenate([beside(lefts[d], order=order) for d in range(count)], axis=1)
    out[...] = fold(jnp.dot(left, wide, preferred_element_type=F32), 1)
    per = cand[0].shape[0]
    for target in range(TARGETS):
        for c in range(4):

            @pl.when(info[target] == c)
            def _():
                for h in range(halves):
                    chosen[target, h * per : (h + 1) * per] = cand[c * halves + h][...]


def final_body(count, parts, info, *refs):
    weights = refs[:parts]
    sketch, chosen, factor, basis, update, total = refs[parts:]
    cap = factor.shape[-1]
    tall = basis.shape[1] * count
    side = info[1]
    acc = weights[0][...]
    if parts > 1:
        acc = jnp.where(info[0] == 0, acc, 0.0)
    for d in range(1, parts):
        acc += weights[d][...]
    total[...] = acc
    for target in range(TARGETS):
        cols = slice(target * cap, (target + 1) * cap)
        lefts, heads = [], []
        for d in range(count):
            at = lax.rem(info[0] + d, count) * PAIR
            for l in range(PAIR):
                heads.append(total[at + l, cols, :])
                lefts.append(chosen[target, d * PAIR + (1 - side if l else side)])
        top, low = split(jnp.concatenate(heads, axis=1))
        got = dot1(jnp.concatenate(lefts, axis=1), jnp.concatenate([top, low], axis=0))
        inverse = factor[target]
        basis[0, :, target, :] = dot1(sketch[:, cols], inverse, HIGH)
        update[0, :, target, :] = dot1(fold(got, 1), inverse, HIGH) * (1.0 / tall)


def steps(panel_left, panel_right, test_matrix, ranks, offsets):
    n, m = lax.axis_size("row"), lax.axis_size("layer")
    tall, cap = panel_left.shape[2:]
    share = tall // m
    span = TARGETS * cap
    row, z = lax.axis_index("row"), lax.axis_index("layer")
    j = row % PAIR
    roots = [m // 2 - 1 + side for side in range(PAIR)]
    my_root = jnp.where(j == 0, roots[0], roots[1])
    is_root = z == my_root

    def array(shape, dtype=F32):
        return jax.ShapeDtypeStruct(shape, dtype)

    def along(x, shift):
        return lax.ppermute(x, "row", [(i, (i + shift) % n) for i in range(n)])

    def swap(x):
        return lax.ppermute(x, "row", [(i, i ^ 1) for i in range(n)])

    relay = n == 2 * FRONTS

    def group_before(own, two_before):
        if relay:
            sent = jnp.where((row // PAIR) % 2 == 1, two_before, own)
            return lax.ppermute(sent, "row", [(i, i ^ PAIR) for i in range(n)])
        return along(own, PAIR)

    def flat(x, pairs):
        return lax.ppermute(x, ("row", "layer"), [(a * m + b, c * m + d) for a, b, c, d in pairs])

    def to_root(x, d):
        pairs = [(r, (roots[r % PAIR] + d) % m, r, roots[r % PAIR]) for r in range(n)]
        return flat(x, pairs)

    def to_rest(x, d):
        pairs = [
            (r, (k + d) % m, r, k) for r in range(n) for k in range(m) if k != roots[r % PAIR]
        ]
        return flat(x, pairs)

    def from_root(x, d):
        pairs = [(r, roots[r % PAIR], r, (roots[r % PAIR] + d) % m) for r in range(n)]
        return flat(x, pairs)

    def doubled(x):
        x = jnp.where(is_root, x, 0.0)
        width = 1
        while width < m:
            reach = range(min(width, m - width))
            ends = [(roots[r % PAIR] + e, r) for r in range(n) for e in reach]
            x = x + flat(x, [(r, k % m, r, (k + width) % m) for k, r in ends])
            width *= 2
        return x

    others = range(1, m)
    left, right = panel_left[0], panel_right[0]
    j_arr = j[None].astype(jnp.int32)

    tile = array((tall, cap), BF16)
    v_own, v_oth = call(
        mask_body, (tile, tile), [jnp.concatenate([ranks[0], j_arr]), right], smem=1
    )
    v_sib = swap(v_oth)
    vy_own = along(v_own, FRONTS)

    def piece(at):
        return lax.dynamic_slice_in_dim(left, at * share, share, 1)

    everyone = [(r, k) for r in range(n) for k in range(m)]
    u_rows = [piece(z)] + [
        flat(piece((z - d) % m), [(r, (k + d) % m, r, k) for r, k in everyone])
        for d in others
    ]
    p_own, message = call(
        probe_body,
        (array((cap, cap)), array((cap + 8, cap))),
        [jnp.concatenate([offsets[0], j_arr]), left, test_matrix],
        smem=1,
    )
    vy_sib = along(v_sib, FRONTS)
    got = swap(message)
    u_root = [left] + [to_root(left, d) for d in others]
    p_pair = jnp.stack([p_own, got[:cap]])
    py = along(p_pair, FRONTS)
    vx_own = group_before(v_own, vy_own)
    px = group_before(p_pair, py)
    vx_sib = group_before(v_sib, vy_sib)

    def back(steps, side):
        v = steps - side
        return (v + 1) // PAIR, v % PAIR

    sib_offsets = got[cap : cap + 1, :TARGETS].astype(jnp.int32)
    own_group, own_core = back(offsets[0], j)
    sib_group, sib_core = back(sib_offsets[0], 1 - j)
    idx = jnp.concatenate(
        [
            PAIR * own_group + (own_core != j).astype(jnp.int32),
            PAIR * sib_group + (sib_core != j).astype(jnp.int32),
        ]
    ).astype(jnp.int32)

    halves = 2
    u_half = [
        jnp.concatenate(u_rows[h * m // halves : (h + 1) * m // halves], axis=0)
        for h in range(halves)
    ]
    uy = [along(u, FRONTS) for u in u_half]

    block = array((cap, span))
    mix_own, mix_sib, core_own, core_sib = call(
        core_body,
        (block,) * 4,
        [idx, v_own, v_sib, vx_own, vx_sib, vy_own, vy_sib, p_own, got, px, py],
        [pltpu.VMEM((PAIR, 6, cap, cap), F32), pltpu.VMEM((6, cap, cap), F32)],
        smem=1,
    )
    mix = jnp.stack([mix_own, swap(mix_sib)])
    mix_root = [mix] + [to_root(mix, d) for d in others]
    core = jnp.stack([core_own, swap(core_sib)])
    core_root = [core] + [to_root(core, d) for d in others]
    ux = [group_before(u, y) for u, y in zip(u_half, uy)]
    mix_rest = [to_rest(mix, d) for d in others]

    sketch, gram = call(
        functools.partial(sketch_body, m),
        (array((tall, 2 * span), BF16), array((TARGETS, cap, cap))),
        [j_arr, *u_root, *mix_root],
        [pltpu.VMEM((m * PAIR * cap, 2 * span), BF16), pltpu.VMEM((tall, span), F32)],
        smem=1,
    )
    weights = call(
        functools.partial(weight_body, m),
        array((m * PAIR, span, cap)),
        [j_arr, *u_root, *core_root, sketch],
        smem=1,
    )
    if m <= MOST:
        weight_all = [weights] + [from_root(weights, d) for d in others]
    else:
        weight_all = [doubled(weights)]
    gram_all = [jnp.where(is_root, gram, 0.0)] + [from_root(gram, d) for d in others]

    first = [swap(jnp.where(j == 0, u, y)) for u, y in zip(u_half, uy)]
    second = [swap(x) for x in ux]
    pick = jnp.where(own_core == j, own_group - 1, jnp.where(own_group == 1, 3, 2))
    sketch_rows, chosen = call(
        functools.partial(slice_body, m, halves),
        (array((share, span)), array((TARGETS, m * PAIR, share, cap), BF16)),
        [
            jnp.concatenate([pick.astype(jnp.int32), j_arr]),
            *u_rows,
            *mix_root,
            *mix_rest,
            *ux,
            *uy,
            *first,
            *second,
        ],
        smem=1,
    )
    factor = call(
        functools.partial(factor_body, m),
        array((TARGETS, cap, cap)),
        gram_all,
        [pltpu.VMEM((TARGETS, cap, 2 * cap), F32)],
    )
    place = jnp.stack([(z - my_root) % m, j]).astype(jnp.int32)
    out = array((1, share, TARGETS, cap))
    return call(
        functools.partial(final_body, m, len(weight_all)),
        (out, out),
        [place, *weight_all, sketch_rows, chosen, factor],
        [pltpu.VMEM((m * PAIR, span, cap), F32)],
        smem=1,
    )


def solution(mesh):
    return jax.shard_map(
        steps,
        mesh=mesh,
        in_specs=(
            P("row", "layer", None, None),
            P("row", "layer", None, None),
            P(),
            P("row", "layer"),
            P("row", None),
        ),
        out_specs=(P("row", "layer", None, None), P("row", "layer", None, None)),
        check_vma=False,
    )
```

```python
import functools

import jax
import jax.numpy as jnp
from jax import lax
from jax.experimental import pallas as pl
from jax.experimental.pallas import tpu as pltpu
from jax.sharding import PartitionSpec as P


FRONTS = 4
TARGETS = 2
PAIR = 2
MOST = 4
HIGH = lax.Precision.HIGHEST
F32 = jnp.float32
BF16 = jnp.bfloat16


def dot0(a, b, precision=None):
    return lax.dot_general(
        a, b, (((0,), (0,)), ((), ())), precision=precision, preferred_element_type=F32
    )


def dot1(a, b, precision=None):
    return lax.dot_general(
        a, b, (((1,), (1,)), ((), ())), precision=precision, preferred_element_type=F32
    )


def split(x):
    top = x.astype(BF16)
    return top, (x - top.astype(F32)).astype(BF16)


def fold(x, axis):
    first, second = jnp.split(x, 2, axis)
    return first + second


def beside(ref, rows=slice(None), order=(0, 1)):
    return jnp.concatenate([ref[order[0], rows, :], ref[order[1], rows, :]], axis=1)


SMALL = 12 << 20


def call(body, outs, args, scratch=(), smem=0, grant=12 << 20):
    size = sum(a.size * a.dtype.itemsize for a in args)
    size += sum(o.size * o.dtype.itemsize for o in jax.tree.leaves(outs))
    keep = size <= SMALL
    specs = [pl.BlockSpec(memory_space=pltpu.SMEM)] * smem
    specs += [pl.BlockSpec(memory_space=pltpu.VMEM)] * (len(args) - smem)
    if keep:
        args = [
            a if i < smem else pltpu.with_memory_space_constraint(a, pltpu.VMEM)
            for i, a in enumerate(args)
        ]
    return pl.pallas_call(
        body,
        out_shape=outs,
        in_specs=specs,
        out_specs=jax.tree.map(lambda _: pl.BlockSpec(memory_space=pltpu.VMEM), outs),
        scratch_shapes=list(scratch),
        compiler_params=pltpu.CompilerParams(vmem_limit_bytes=grant if keep else 56 << 20),
    )(*args)


def mask_body(info, right, own, other):
    cap = right.shape[-1]
    lane = lax.broadcasted_iota(jnp.int32, (1, cap), 1)
    side = info[PAIR]
    for out, layer in ((own, side), (other, 1 - side)):
        live = (lane < info[layer]).astype(F32).astype(BF16)
        out[...] = right[layer] * live


def probe_body(info, left, test, own, message):
    cap = left.shape[-1]
    side = info[TARGETS]
    own[...] = dot0(left[side], test[...])
    message[:cap] = dot0(left[1 - side], test[...])
    lane = lax.broadcasted_iota(jnp.int32, (8, cap), 1)
    note = jnp.zeros((8, cap), F32)
    for target in range(TARGETS):
        note = jnp.where(lane == target, info[target].astype(F32), note)
    message[cap:] = note


def choose_body(flag, no, yes, out):
    @pl.when(flag[0] == 0)
    def _():
        out[...] = no[...]

    @pl.when(flag[0] != 0)
    def _():
        out[...] = yes[...]


def pack_body(count, *refs):
    parts, outs = refs[:count], refs[count:]
    per = count // len(outs)
    wide = parts[0].shape[0]
    for k in range(count):
        spot = (k % per) * wide
        outs[k // per][spot : spot + wide] = parts[k][...]


def pair_body(own, other, mix, core):
    for out, kind in ((mix, 0), (core, 1)):
        out[0] = own[kind]
        out[1] = other[kind]


def core_body(idx, v0, v1, x0, x1, y0, y1, p0, p1, px, py, *rest):
    outs, (cores, probes) = rest[:2], rest[2:]
    cap = v0.shape[-1]
    both = jnp.concatenate([v0[...], v1[...]], axis=1)
    inner = dot0(v0[...], v1[...])
    cores[0, 1] = inner
    cores[1, 0] = inner.T
    for slot, (left, right) in ((4, (y0, y1)), (2, (x0, x1))):
        prod = dot0(both, jnp.concatenate([left[...], right[...]], axis=1))
        for owner in range(PAIR):
            for side in range(PAIR):
                cores[owner, slot + side] = prod[
                    owner * cap : (owner + 1) * cap, side * cap : (side + 1) * cap
                ]
    probes[0] = p0[...]
    probes[1] = p1[:cap, :]
    for side in range(PAIR):
        probes[2 + side] = px[side]
        probes[4 + side] = py[side]
    for owner in range(PAIR):
        for target in range(TARGETS):
            tile = idx[owner * TARGETS + target]
            core = cores[owner, tile]
            cols = slice(target * cap, (target + 1) * cap)
            outs[owner][1, :, cols] = core
            outs[owner][0, :, cols] = jnp.dot(
                core, probes[tile], precision=HIGH, preferred_element_type=F32
            )


def sketch_body(count, info, *refs):
    lefts, mixers = refs[:count], refs[count : 2 * count]
    out, gram, wide, whole = refs[2 * count :]
    side = info[0]
    order = (side, 1 - side)
    cap = lefts[0].shape[-1]
    tall = lefts[0].shape[1]
    span = TARGETS * cap
    block = min(512, tall)
    for d in range(count):
        for l in range(PAIR):
            rows = slice((PAIR * d + l) * cap, (PAIR * d + l + 1) * cap)
            wide[rows, :span], wide[rows, span:] = split(mixers[d][l])
    for first in range(0, tall, block):
        rows = slice(first, first + block)
        left = jnp.concatenate([beside(lefts[d], rows, order) for d in range(count)], axis=1)
        sketch = fold(jnp.dot(left, wide[...], preferred_element_type=F32), 1)
        out[rows, :span], out[rows, span:] = split(sketch)
        whole[rows, :] = sketch
    for target in range(TARGETS):
        piece = whole[:, target * cap : (target + 1) * cap]
        top, mid = split(piece)
        low = (piece - top.astype(F32) - mid.astype(F32)).astype(BF16)
        near = jnp.concatenate([top, mid], axis=1)
        prod = dot0(near, near)
        cross = prod[:cap, cap:] + dot0(top, low)
        cross = cross + cross.T
        gram[target] = (prod[:cap, :cap] + (cross + prod[cap:, cap:])) * (1.0 / tall)


def weight_body(count, info, *refs):
    lefts, cores = refs[:count], refs[count : 2 * count]
    sketch, out = refs[2 * count :]
    side = info[0]
    cap = lefts[0].shape[-1]
    for d in range(count):
        reach = fold(dot0(sketch[...], beside(lefts[d], order=(side, 1 - side))), 0)
        for l in range(PAIR):
            for target in range(TARGETS):
                cols = slice(target * cap, (target + 1) * cap)
                a0, a1 = split(reach[cols, l * cap : (l + 1) * cap])
                b0, b1 = split(cores[d][l, :, cols])
                out[d * PAIR + l, cols, :] = jnp.dot(
                    jnp.concatenate([a0, a0, a1], axis=1),
                    jnp.concatenate([b0, b1, b0], axis=0),
                    preferred_element_type=F32,
                )


def factor_body(count, *refs):
    grams, (out, work) = refs[:count], refs[count:]
    cap = out.shape[-1]
    panel = 16
    lane = lax.broadcasted_iota(jnp.int32, (cap, cap), 1)
    line = lax.broadcasted_iota(jnp.int32, (cap, cap), 0)
    for target in range(TARGETS):
        gram = grams[0][target]
        for other in grams[1:]:
            gram = gram + other[target]
        work[target, :, :cap] = gram
        work[target, :, cap:] = (lane == line).astype(F32)
    place = lax.broadcasted_iota(jnp.int32, (panel, 1), 0)
    for first in range(0, cap, panel):
        rows = [work[target, first : first + panel, :] for target in range(TARGETS)]
        for i in range(panel):
            for target in range(TARGETS):
                column = rows[target][:, first + i : first + i + 1]
                inv = lax.rsqrt(column[i : i + 1, :])
                line_i = rows[target][i : i + 1, :] * inv
                below = jnp.where(place > i, column * inv, 0.0)
                rows[target] = jnp.where(place == i, line_i, rows[target] - below * line_i)
        for target in range(TARGETS):
            out[target, first : first + panel, :] = rows[target][:, cap:]
            if first + panel < cap:
                tail = slice(first + panel, cap)
                work[target, tail, :] = work[target, tail, :] - dot0(
                    rows[target][:, tail], rows[target], HIGH
                )


def slice_body(count, halves, info, *refs):
    lefts = refs[:count]
    roots = refs[count : 2 * count]
    rests = refs[2 * count : 3 * count - 1]
    cand = refs[3 * count - 1 : 3 * count - 1 + 4 * halves]
    out, chosen = refs[3 * count - 1 + 4 * halves :]
    side = info[TARGETS]
    order = (side, 1 - side)
    parts = []
    for d in range(count):
        mix = roots[d][...] if d == 0 else roots[d][...] + rests[d - 1][...]
        parts.append(jnp.concatenate([mix[0], mix[1]], axis=0))
    wide = jnp.concatenate(split(jnp.concatenate(parts, axis=0)), axis=1)
    left = jnp.concatenate([beside(lefts[d], order=order) for d in range(count)], axis=1)
    out[...] = fold(jnp.dot(left, wide, preferred_element_type=F32), 1)
    per = cand[0].shape[0]
    for target in range(TARGETS):
        for c in range(4):

            @pl.when(info[target] == c)
            def _():
                for h in range(halves):
                    chosen[target, h * per : (h + 1) * per] = cand[c * halves + h][...]


def final_body(count, parts, info, *refs):
    weights = refs[:parts]
    sketch, chosen, factor, basis, update, total = refs[parts:]
    cap = factor.shape[-1]
    tall = basis.shape[1] * count
    side = info[1]
    acc = weights[0][...]
    if parts > 1:
        acc = jnp.where(info[0] == 0, acc, 0.0)
    for d in range(1, parts):
        acc += weights[d][...]
    total[...] = acc
    for target in range(TARGETS):
        cols = slice(target * cap, (target + 1) * cap)
        lefts, heads = [], []
        for d in range(count):
            at = lax.rem(info[0] + d, count) * PAIR
            for l in range(PAIR):
                heads.append(total[at + l, cols, :])
                lefts.append(chosen[target, d * PAIR + (1 - side if l else side)])
        top, low = split(jnp.concatenate(heads, axis=1))
        got = dot1(jnp.concatenate(lefts, axis=1), jnp.concatenate([top, low], axis=0))
        inverse = factor[target]
        basis[0, :, target, :] = dot1(sketch[:, cols], inverse, HIGH)
        update[0, :, target, :] = dot1(fold(got, 1), inverse, HIGH) * (1.0 / tall)


def steps(panel_left, panel_right, test_matrix, ranks, offsets):
    n, m = lax.axis_size("row"), lax.axis_size("layer")
    tall, cap = panel_left.shape[2:]
    share = tall // m
    span = TARGETS * cap
    row, z = lax.axis_index("row"), lax.axis_index("layer")
    j = row % PAIR
    roots = [m // 2 - 1 + side for side in range(PAIR)]
    my_root = jnp.where(j == 0, roots[0], roots[1])
    is_root = z == my_root

    def array(shape, dtype=F32):
        return jax.ShapeDtypeStruct(shape, dtype)

    def along(x, shift):
        return lax.ppermute(x, "row", [(i, (i + shift) % n) for i in range(n)])

    def swap(x):
        return lax.ppermute(x, "row", [(i, i ^ 1) for i in range(n)])

    relay = n == 2 * FRONTS

    def group_before(own, two_before):
        if relay:
            odd = (row // PAIR) % 2
            if own.dtype == BF16:
                out = array(own.shape, BF16)
                sent = call(choose_body, out, [odd[None], own, two_before], smem=1)
            else:
                sent = jnp.where(odd == 1, two_before, own)
            return lax.ppermute(sent, "row", [(i, i ^ PAIR) for i in range(n)])
        return along(own, PAIR)

    def flat(x, pairs):
        return lax.ppermute(x, ("row", "layer"), [(a * m + b, c * m + d) for a, b, c, d in pairs])

    def to_root(x, d):
        pairs = [(r, (roots[r % PAIR] + d) % m, r, roots[r % PAIR]) for r in range(n)]
        return flat(x, pairs)

    def to_rest(x, d):
        pairs = [
            (r, (k + d) % m, r, k) for r in range(n) for k in range(m) if k != roots[r % PAIR]
        ]
        return flat(x, pairs)

    def from_root(x, d):
        pairs = [(r, roots[r % PAIR], r, (roots[r % PAIR] + d) % m) for r in range(n)]
        return flat(x, pairs)

    def doubled(x):
        x = jnp.where(is_root, x, 0.0)
        width = 1
        while width < m:
            reach = range(min(width, m - width))
            ends = [(roots[r % PAIR] + e, r) for r in range(n) for e in reach]
            x = x + flat(x, [(r, k % m, r, (k + width) % m) for k, r in ends])
            width *= 2
        return x

    others = range(1, m)
    left, right = panel_left[0], panel_right[0]
    j_arr = j[None].astype(jnp.int32)

    tile = array((tall, cap), BF16)
    v_own, v_oth = call(
        mask_body, (tile, tile), [jnp.concatenate([ranks[0], j_arr]), right], smem=1
    )
    v_sib = swap(v_oth)
    vy_own = along(v_own, FRONTS)

    def piece(at):
        return lax.dynamic_slice_in_dim(left, at * share, share, 1)

    everyone = [(r, k) for r in range(n) for k in range(m)]
    u_rows = [piece(z)] + [
        flat(piece((z - d) % m), [(r, (k + d) % m, r, k) for r, k in everyone])
        for d in others
    ]
    p_own, message = call(
        probe_body,
        (array((cap, cap)), array((cap + 8, cap))),
        [jnp.concatenate([offsets[0], j_arr]), left, test_matrix],
        smem=1,
    )
    vy_sib = along(v_sib, FRONTS)
    got = swap(message)
    u_root = [left] + [to_root(left, d) for d in others]
    p_pair = jnp.stack([p_own, got[:cap]])
    py = along(p_pair, FRONTS)
    vx_own = group_before(v_own, vy_own)
    px = group_before(p_pair, py)
    vx_sib = group_before(v_sib, vy_sib)

    def back(steps, side):
        v = steps - side
        return (v + 1) // PAIR, v % PAIR

    sib_offsets = got[cap : cap + 1, :TARGETS].astype(jnp.int32)
    own_group, own_core = back(offsets[0], j)
    sib_group, sib_core = back(sib_offsets[0], 1 - j)
    idx = jnp.concatenate(
        [
            PAIR * own_group + (own_core != j).astype(jnp.int32),
            PAIR * sib_group + (sib_core != j).astype(jnp.int32),
        ]
    ).astype(jnp.int32)

    halves = 2
    half = array((m * PAIR // halves, share, cap), BF16)
    u_half = call(functools.partial(pack_body, m), (half,) * halves, u_rows)
    uy = [along(u, FRONTS) for u in u_half]

    block = array((2, cap, span))
    pair_own, pair_sib = call(
        core_body,
        (block,) * 2,
        [idx, v_own, v_sib, vx_own, vx_sib, vy_own, vy_sib, p_own, got, px, py],
        [pltpu.VMEM((PAIR, 6, cap, cap), F32), pltpu.VMEM((6, cap, cap), F32)],
        smem=1,
    )
    mix, core = call(pair_body, (block,) * 2, [pair_own, swap(pair_sib)])
    mix_root = [mix] + [to_root(mix, d) for d in others]
    core_root = [core] + [to_root(core, d) for d in others]
    ux = [group_before(u, y) for u, y in zip(u_half, uy)]
    mix_rest = [to_rest(mix, d) for d in others]

    sketch, gram = call(
        functools.partial(sketch_body, m),
        (array((tall, 2 * span), BF16), array((TARGETS, cap, cap))),
        [j_arr, *u_root, *mix_root],
        [pltpu.VMEM((m * PAIR * cap, 2 * span), BF16), pltpu.VMEM((tall, span), F32)],
        smem=1,
    )
    weights = call(
        functools.partial(weight_body, m),
        array((m * PAIR, span, cap)),
        [j_arr, *u_root, *core_root, sketch],
        smem=1,
    )
    if m <= MOST:
        weight_all = [weights] + [from_root(weights, d) for d in others]
    else:
        weight_all = [doubled(weights)]
    gram_all = [jnp.where(is_root, gram, 0.0)] + [from_root(gram, d) for d in others]

    first = [swap(jnp.where(j == 0, u, y)) for u, y in zip(u_half, uy)]
    second = [swap(x) for x in ux]
    pick = jnp.where(own_core == j, own_group - 1, jnp.where(own_group == 1, 3, 2))
    sketch_rows, chosen = call(
        functools.partial(slice_body, m, halves),
        (array((share, span)), array((TARGETS, m * PAIR, share, cap), BF16)),
        [
            jnp.concatenate([pick.astype(jnp.int32), j_arr]),
            *u_rows,
            *mix_root,
            *mix_rest,
            *ux,
            *uy,
            *first,
            *second,
        ],
        smem=1,
    )
    factor = call(
        functools.partial(factor_body, m),
        array((TARGETS, cap, cap)),
        gram_all,
        [pltpu.VMEM((TARGETS, cap, 2 * cap), F32)],
    )
    place = jnp.stack([(z - my_root) % m, j]).astype(jnp.int32)
    out = array((1, share, TARGETS, cap))
    return call(
        functools.partial(final_body, m, len(weight_all)),
        (out, out),
        [place, *weight_all, sketch_rows, chosen, factor],
        [pltpu.VMEM((m * PAIR, span, cap), F32)],
        smem=1,
    )


def solution(mesh):
    return jax.shard_map(
        steps,
        mesh=mesh,
        in_specs=(
            P("row", "layer", None, None),
            P("row", "layer", None, None),
            P(),
            P("row", "layer"),
            P("row", None),
        ),
        out_specs=(P("row", "layer", None, None), P("row", "layer", None, None)),
        check_vma=False,
    )
```
